256 devices in a mesh: expert: 64 (over x, z, core), dp: 4 (over y).
Axes of the slice: x: 4, y: 4, z: 8, core: 2. Of those that a mesh axis runs over, the one named last changes fastest.
Arguments:
- enc_state: bfloat16 [4, 64, 256, 1024], P('dp', 'expert'), may hold values from -6 to 6
- baseline: bfloat16 [4, 64, 256, 1024], P('dp', 'expert'), may hold values from -6 to 6
- enc_keys: bfloat16 [4, 64, 256, 1024], P('dp', 'expert'), may hold values from -4 to 4
- dec_queries: bfloat16 [4, 64, 128, 1024], P('dp', 'expert'), may hold values from -200 to 200
- out_mult: bfloat16 [4, 64, 128, 1024], P('dp', 'expert'), may hold values from -6 to 6
- doc_lengths: int32 [4, 64], P('dp', 'expert'), may hold values from 128 to 256, as said below
- expert_ids: int32 [4, 64, 256], P('dp', 'expert'), may hold values from 0 to 127
- slot_ids: int32 [4, 64, 256], P('dp', 'expert'), may hold values from 0 to 3, as said below
- gate_prob: float32 [4, 64, 256], P('dp', 'expert'), may hold values from 0.2 to 1
- norm_gain: float32 [1024], replicated, may hold values from 0.5 to 2
- w_in: bfloat16 [128, 1024, 2816], P('expert', None, 'dp'), may hold values from -0.1875 to 0.1875
- w_out_t: bfloat16 [128, 1024, 2816], P('expert', None, 'dp'), may hold values from -0.109375 to 0.109375
- w_value: bfloat16 [1024, 1024], replicated, may hold values from -0.1875 to 0.1875
Outputs:
- enc_mult: bfloat16 [4, 64, 256, 1024], P('dp', 'expert')
The draws below stay inside these ranges and needn't reach their ends.
Inputs may be any that keep to these rules, and one draw needn't show every extreme that they name: `slot_ids`: within one document no two tokens share an expert and a slot, and every token has a slot; one expert has all 4 slots used in every document. `doc_lengths`: some document has all 256 tokens.
All inputs are finite; a program needn't handle non-finite values.
Results may differ from the reference program's by a relative error of at most 0.0069.
Values may be sent and summed in bfloat16 or wider, within the bound.
No kernel may reach another device: no remote copies, remote signals or barrier semaphores. Data moves between devices by JAX's collectives and lax.ppermute only.
A program may use at most 128 MiB of HBM per device.

```python
import math
import jax
import jax.numpy as jnp
from jax import lax

D = 1024
FF = 2816
HEADS = 16
HEAD_DIM = 64
ENC_LEN = 256
DEC_LEN = 128
EXPERTS = 128
CAP = 4
GROUPS = 4
DOC_GRP = 64


def routing_draw(key):
    levels = jax.random.randint(jax.random.fold_in(key, 101), (EXPERTS,), 0, 4)
    busiest = jax.random.randint(jax.random.fold_in(key, 102), (), 0, EXPERTS)
    levels = jnp.where(jnp.arange(EXPERTS) == busiest, 9, levels)
    jitter = jax.random.randint(jax.random.fold_in(key, 103), (GROUPS, DOC_GRP, EXPERTS, CAP), 0, 3072)
    scores = (levels[:, None] * 1024 + jitter).reshape(GROUPS, DOC_GRP, EXPERTS * CAP)
    ranked = jnp.argsort(-scores, axis=-1, stable=True)[:, :, :ENC_LEN]
    shuffle_keys = jax.random.randint(jax.random.fold_in(key, 104), (GROUPS, DOC_GRP, ENC_LEN), 0, 2 ** 30)
    shuffle = jnp.argsort(shuffle_keys, axis=-1, stable=True)
    chosen = jnp.take_along_axis(ranked, shuffle, axis=-1)
    return ((chosen // CAP).astype(jnp.int32), (chosen % CAP).astype(jnp.int32))


def attention_draw(key):
    keys = jnp.clip(jax.random.normal(jax.random.fold_in(key, 201), (GROUPS, DOC_GRP, ENC_LEN, D), jnp.float32), -4.0, 4.0)
    queries = 0.5 * jnp.clip(jax.random.normal(jax.random.fold_in(key, 202), (GROUPS, DOC_GRP, DEC_LEN, D), jnp.float32), -6.0, 6.0)
    return (keys, queries)


def draw_enc_keys(key, part):
    return attention_draw(key)[0].astype(jnp.bfloat16)


def draw_dec_queries(key, part):
    return attention_draw(key)[1].astype(jnp.bfloat16)


def draw_doc_lengths(key, part):
    doc_len = jax.random.randint(jax.random.fold_in(key, 301), (GROUPS, DOC_GRP), ENC_LEN // 2, ENC_LEN + 1)
    full_doc = jax.random.randint(jax.random.fold_in(key, 302), (), 0, GROUPS * DOC_GRP)
    doc_index = jnp.arange(GROUPS * DOC_GRP).reshape(GROUPS, DOC_GRP)
    return jnp.where(doc_index == full_doc, ENC_LEN, doc_len).astype(jnp.int32)


def draw_expert_ids(key, part):
    return routing_draw(key)[0]


def draw_slot_ids(key, part):
    return routing_draw(key)[1]


def block_scale(stream_key, dims, shards, least, top_value):
    loudness, own = 1.0, jax.random.fold_in(stream_key, 6)
    for axis_at, shards_of in shards:
        heights = jnp.exp(jax.random.uniform(jax.random.fold_in(own, axis_at), (shards_of,), jnp.float32, least / len(shards), top_value / len(shards)))
        loudness = loudness * jnp.repeat(heights, dims[axis_at] // shards_of).reshape([-1 if axis == axis_at else 1 for axis in range(len(dims))])
    return loudness


def normal_values(own_key, shape, deviation, reach, cuts=(), held_as=jnp.bfloat16):
    factor_of = block_scale(own_key, shape, cuts, -0.22, 0.18) if cuts else 1.0
    values = jax.random.normal(own_key, shape, jnp.float32) * deviation * factor_of
    return jnp.minimum(jnp.maximum(values, -reach), reach).astype(held_as)


def setup_inputs(seed: int = 0) -> dict:
    streams_of = jax.random.split(jax.random.key(seed), 14)
    return {
        "enc_state": normal_values(streams_of[0], (GROUPS, DOC_GRP, ENC_LEN, D), 1.0, 6.0, ((0, 4), (1, 64))),
        "baseline": normal_values(streams_of[1], (GROUPS, DOC_GRP, ENC_LEN, D), 1.0, 6.0, ((0, 4), (1, 64))),
        "enc_keys": draw_enc_keys(jax.random.fold_in(streams_of[13], 71), 0),
        "dec_queries": draw_dec_queries(jax.random.fold_in(streams_of[13], 71), 0),
        "out_mult": normal_values(streams_of[4], (GROUPS, DOC_GRP, DEC_LEN, D), 1.0, 6.0, ((0, 4), (1, 64))),
        "doc_lengths": draw_doc_lengths(jax.random.fold_in(streams_of[13], 71), 0),
        "expert_ids": draw_expert_ids(jax.random.fold_in(streams_of[13], 71), 0),
        "slot_ids": draw_slot_ids(jax.random.fold_in(streams_of[13], 71), 0),
        "gate_prob": jnp.clip(jnp.exp(math.log(1.0) - 1.609438 * jax.random.uniform(streams_of[8], (GROUPS, DOC_GRP, ENC_LEN), jnp.float32) ** block_scale(streams_of[8], (GROUPS, DOC_GRP, ENC_LEN), ((0, 4), (1, 64)), -0.2, 0.2)), 0.2, 1.0),
        "norm_gain": jnp.clip(jnp.exp(jax.random.uniform(streams_of[9], (D,), jnp.float32, math.log(0.5), math.log(2.0))), 0.5, 2.0),
        "w_in": normal_values(streams_of[10], (EXPERTS, D, FF), D ** -0.5, 0.1875, ((0, 64), (2, 4))),
        "w_out_t": normal_values(streams_of[11], (EXPERTS, D, FF), FF ** -0.5, 0.109375, ((0, 64), (2, 4))),
        "w_value": normal_values(streams_of[12], (D, D), D ** -0.5, 0.1875),
    }


def rescale(pre_act, base_act):
    upper_part = jnp.maximum(jnp.maximum(pre_act, base_act), 0.0)
    lower_part = jnp.maximum(-jnp.minimum(pre_act, base_act), 0.0)
    return upper_part / (upper_part + lower_part + jnp.where(upper_part > 0.0, 0.0, 1.0))

def attend(query_rows, key_rows, mult_rows, length, w_value):
    enc_len = key_rows.shape[0]
    dec_len = query_rows.shape[0]
    queries = query_rows.astype(jnp.float32).reshape(dec_len, HEADS, HEAD_DIM)
    keys = key_rows.astype(jnp.float32).reshape(enc_len, HEADS, HEAD_DIM)
    mults = mult_rows.astype(jnp.float32).reshape(dec_len, HEADS, HEAD_DIM)
    scores = jnp.einsum('qhd,khd->hqk', queries, keys) * (1.0 / math.sqrt(HEAD_DIM))
    valid = jnp.arange(enc_len, dtype=jnp.int32) < length
    scores = jnp.where(valid[None, None, :], scores, -jnp.inf)
    top_score = lax.optimization_barrier(jnp.max(scores, axis=-1, keepdims=True))
    expo = jnp.exp(scores - top_score)
    attn = (expo / lax.optimization_barrier(jnp.sum(expo, axis=-1, keepdims=True))).astype(jnp.bfloat16)
    value_mult = jnp.einsum('hqk,qhd->khd', attn.astype(jnp.float32), mults).astype(jnp.bfloat16)
    return jnp.dot(value_mult.reshape(enc_len, HEADS * HEAD_DIM), w_value.T, preferred_element_type=jnp.float32)

def reference(enc_state, baseline, enc_keys, dec_queries, out_mult, doc_lengths, expert_ids, slot_ids, gate_prob, norm_gain, w_in, w_out_t, w_value):
    n_docs = GROUPS * DOC_GRP
    flat_queries = dec_queries.reshape(n_docs, DEC_LEN, D)
    flat_keys = enc_keys.reshape(n_docs, ENC_LEN, D)
    flat_mults = out_mult.reshape(n_docs, DEC_LEN, D)
    flat_len = doc_lengths.reshape(n_docs)
    layer_mult = lax.map(lambda item: attend(item[0], item[1], item[2], item[3], w_value), (flat_queries, flat_keys, flat_mults, flat_len))
    tokens = enc_state.reshape(n_docs, ENC_LEN, D).astype(jnp.float32)
    row_scale = norm_gain.astype(jnp.float32) * lax.rsqrt(lax.optimization_barrier(jnp.mean(tokens * tokens, axis=-1, keepdims=True)) + 1e-06)
    inputs = (tokens * row_scale).astype(jnp.bfloat16)
    base_inputs = (baseline.reshape(n_docs, ENC_LEN, D).astype(jnp.float32) * row_scale).astype(jnp.bfloat16)
    scaled_mult = (gate_prob.reshape(n_docs, ENC_LEN, 1).astype(jnp.float32) * layer_mult).astype(jnp.bfloat16)
    doc_index = jnp.broadcast_to(jnp.arange(n_docs, dtype=jnp.int32)[:, None], (n_docs, ENC_LEN))
    flat_ids = expert_ids.reshape(n_docs, ENC_LEN).astype(jnp.int32)
    flat_slots = slot_ids.reshape(n_docs, ENC_LEN).astype(jnp.int32)

    def place_rows(values):
        filled = jnp.zeros((n_docs, EXPERTS, CAP, D), jnp.bfloat16).at[doc_index, flat_ids, flat_slots].set(values)
        return jnp.swapaxes(filled, 0, 1)
    buf_in = place_rows(inputs)
    buf_base = place_rows(base_inputs)
    buf_mult = place_rows(scaled_mult)

    def one_expert(item):
        weight_in, weight_out, rows_in, rows_base, rows_mult = item
        rows_in = rows_in.reshape(n_docs * CAP, D)
        rows_base = rows_base.reshape(n_docs * CAP, D)
        rows_mult = rows_mult.reshape(n_docs * CAP, D)
        pre_act = jnp.dot(rows_in, weight_in, preferred_element_type=jnp.float32)
        base_act = jnp.dot(rows_base, weight_in, preferred_element_type=jnp.float32)
        hidden_mult = jnp.dot(rows_mult, weight_out, preferred_element_type=jnp.float32)
        act_mult = (rescale(pre_act, base_act) * hidden_mult).astype(jnp.bfloat16)
        slot_mult = jnp.dot(act_mult, weight_in.T, preferred_element_type=jnp.float32).astype(jnp.bfloat16)
        return slot_mult.reshape(n_docs, CAP, D)
    expert_out = lax.map(one_expert, (w_in, w_out_t, buf_in, buf_base, buf_mult))
    per_token = expert_out[flat_ids, doc_index, flat_slots].astype(jnp.float32)
    result = (layer_mult + row_scale * per_token).astype(jnp.bfloat16)
    return result.reshape(GROUPS, DOC_GRP, ENC_LEN, D)
```

```python
import math

import jax
import jax.numpy as jnp
from jax import lax
from jax.experimental import pallas as pl
from jax.experimental.pallas import tpu as pltpu
from jax.sharding import PartitionSpec as P

HEAD_DIM = 64
NT = (((1,), (1,)), ((), ()))
F32 = jnp.float32
BF16 = jnp.bfloat16


def mm(lhs, rhs):
    return jnp.dot(lhs, rhs, preferred_element_type=F32)


def mm_nt(lhs, rhs):
    return lax.dot_general(lhs, rhs, NT, preferred_element_type=F32)


def column_of(row):
    n = row.shape[1]
    eye = lax.broadcasted_iota(jnp.int32, (n, n), 0) == lax.broadcasted_iota(jnp.int32, (n, n), 1)
    return jnp.sum(jnp.where(eye, jnp.broadcast_to(row, (n, n)), 0.0), axis=1, keepdims=True)


def prepare_kernel(
    length_ref, ids_ref, slots_ref, gate_ref, gain_ref, enc_hbm, base_hbm, keys_hbm, query_hbm, mult_hbm, wv_hbm,
    placed_ref, layer_ref, scale_ref,
    enc_ref, base_ref, keys_ref, query_ref, mult_ref, wv_ref, value_ref, sems,
):
    enc_len, width = enc_ref.shape
    dec_len = query_ref.shape[0]
    copies = [
        pltpu.make_async_copy(src, dst, sems.at[i])
        for i, (src, dst) in enumerate(
            (
                (keys_hbm, keys_ref), (query_hbm, query_ref), (mult_hbm, mult_ref),
                (wv_hbm, wv_ref), (enc_hbm, enc_ref), (base_hbm, base_ref),
            )
        )
    ]
    for copy in copies:
        copy.start()
    for copy in copies[:3]:
        copy.wait()
    first = lax.broadcasted_iota(jnp.int32, (dec_len, 2 * HEAD_DIM), 1) < HEAD_DIM
    valid = lax.broadcasted_iota(jnp.int32, (enc_len, 2 * dec_len), 0) < length_ref[0, 0]
    for pair in range(width // (2 * HEAD_DIM)):
        lanes = slice(pair * 2 * HEAD_DIM, (pair + 1) * 2 * HEAD_DIM)
        query, mult = query_ref[:, lanes], mult_ref[:, lanes]
        zeros = jnp.zeros_like(query)
        queries = jnp.concatenate([jnp.where(first, query, zeros), jnp.where(first, zeros, query)], axis=0)
        mults = jnp.concatenate([jnp.where(first, mult, zeros), jnp.where(first, zeros, mult)], axis=0)
        scores = mm_nt(keys_ref[:, lanes], queries) * (1.0 / math.sqrt(HEAD_DIM))
        scores = jnp.where(valid, scores, -jnp.inf)
        expo = jnp.exp(scores - jnp.max(scores, axis=0, keepdims=True))
        attn = (expo * (1.0 / jnp.sum(expo, axis=0, keepdims=True))).astype(BF16)
        value_ref[:, lanes] = mm(attn, mults).astype(BF16)
    copies[3].wait()
    layer_mult = mm_nt(value_ref[...], wv_ref[...])
    layer_ref[...] = layer_mult
    scaled_mult = (column_of(gate_ref[...]) * layer_mult).astype(BF16)
    copies[4].wait()
    copies[5].wait()
    tokens = enc_ref[...].astype(F32)
    inv = lax.rsqrt(jnp.mean(tokens * tokens, axis=-1, keepdims=True) + 1e-06)
    scale_ref[...] = jnp.broadcast_to(inv, scale_ref.shape)
    row_scale = gain_ref[...] * inv
    inputs = (tokens * row_scale).astype(BF16)
    base_inputs = (base_ref[...].astype(F32) * row_scale).astype(BF16)
    half = width // 2
    row = ids_ref[...] * 8 + slots_ref[...]
    at = lax.broadcasted_iota(jnp.int32, (placed_ref.shape[0], enc_len), 0)
    low = jnp.where(at == row, 1.0, 0.0).astype(BF16)
    high = jnp.where(at == row + 4, 1.0, 0.0).astype(BF16)
    placed_ref[:, :half] = (mm(low, inputs[:, :half]) + mm(high, inputs[:, half:])).astype(BF16)
    placed_ref[:, half:width] = (mm(low, base_inputs[:, :half]) + mm(high, base_inputs[:, half:])).astype(BF16)
    placed_ref[:, width:] = (mm(low, scaled_mult[:, :half]) + mm(high, scaled_mult[:, half:])).astype(BF16)


def prepare(length, ids, slots, gate, gain, enc, base, keys, query, mult, wv, n_rows):
    enc_len, width = enc.shape
    any_spec = pl.BlockSpec(memory_space=pl.ANY)
    vmem = pl.BlockSpec(memory_space=pltpu.VMEM)
    return pl.pallas_call(
        prepare_kernel,
        in_specs=[pl.BlockSpec(memory_space=pltpu.SMEM)] + [vmem] * 4 + [any_spec] * 6,
        out_specs=[vmem] * 3,
        out_shape=[
            jax.ShapeDtypeStruct((n_rows, 3 * width // 2), BF16),
            jax.ShapeDtypeStruct((enc_len, width), F32),
            jax.ShapeDtypeStruct((enc_len, 128), F32),
        ],
        scratch_shapes=[pltpu.VMEM(a.shape, BF16) for a in (enc, base, keys, query, mult, wv)]
        + [pltpu.VMEM((enc_len, width), BF16), pltpu.SemaphoreType.DMA((6,))],
        compiler_params=pltpu.CompilerParams(vmem_limit_bytes=48 << 20),
        name="prepare",
    )(length, ids, slots, gate, gain, enc, base, keys, query, mult, wv)


def expert_kernel(rows_ref, *refs, n_parts):
    weights_hbm = refs[: 2 * n_parts]
    out_ref = refs[2 * n_parts]
    weights = refs[2 * n_parts + 1 : 4 * n_parts + 1]
    in_ref, base_ref, mult_ref, acc_ref, sems = refs[4 * n_parts + 1 :]
    copies = [
        pltpu.make_async_copy(weights_hbm[i], weights[i], sems.at[i]) for i in range(2 * n_parts)
    ]
    for copy in copies:
        copy.start()
    n_tiles, _, lanes = rows_ref.shape
    half = lanes // 3
    upper_rows = lax.broadcasted_iota(jnp.int32, (n_tiles // 2, 8, half), 1) < 4
    for i, ref in enumerate((in_ref, base_ref, mult_ref)):
        block = rows_ref[:, :, i * half : (i + 1) * half].astype(F32).reshape(n_tiles // 2, 2, 8, half)
        even, odd = block[:, 0], block[:, 1]
        low = jnp.where(upper_rows, even, pltpu.roll(odd, 4, 1))
        high = jnp.where(upper_rows, pltpu.roll(even, 4, 1), odd)
        ref[:, :half] = low.reshape(n_tiles * 4, half).astype(BF16)
        ref[:, half:] = high.reshape(n_tiles * 4, half).astype(BF16)
    n_rows = n_tiles * 4
    block = n_rows // 2
    for part in range(n_parts):
        copies[2 * part].wait()
        copies[2 * part + 1].wait()
        part_in, part_out = weights[2 * part], weights[2 * part + 1]
        for at in range(0, n_rows, block):
            rows = slice(at, at + block)
            pre_act = mm(in_ref[rows, :], part_in[...])
            base_act = mm(base_ref[rows, :], part_in[...])
            hidden_mult = mm(mult_ref[rows, :], part_out[...])
            upper_part = jnp.maximum(jnp.maximum(pre_act, base_act), 0.0)
            lower_part = jnp.maximum(-jnp.minimum(pre_act, base_act), 0.0)
            ratio = upper_part / (upper_part + lower_part + jnp.where(upper_part > 0.0, 0.0, 1.0))
            term = mm_nt((ratio * hidden_mult).astype(BF16), part_in[...])
            if part == 0:
                acc_ref[rows, :] = term
            else:
                acc_ref[rows, :] += term
    low = acc_ref[:, :half].reshape(n_tiles // 2, 8, half)
    high = acc_ref[:, half:].reshape(n_tiles // 2, 8, half)
    even = jnp.where(upper_rows, low, pltpu.roll(high, 4, 1)).astype(BF16)
    odd = jnp.where(upper_rows, pltpu.roll(low, 4, 1), high).astype(BF16)
    out_ref[:, 0] = even
    out_ref[:, 1] = odd


def expert_terms(rows, parts):
    n_tiles, _, lanes = rows.shape
    half = lanes // 3
    flat = [w for pair in parts for w in pair]
    out = pl.pallas_call(
        lambda *refs: expert_kernel(*refs, n_parts=len(parts)),
        in_specs=[pl.BlockSpec(memory_space=pltpu.VMEM)] + [pl.BlockSpec(memory_space=pl.ANY)] * len(flat),
        out_specs=pl.BlockSpec(memory_space=pltpu.VMEM),
        out_shape=jax.ShapeDtypeStruct((n_tiles // 2, 2, 8, half), BF16),
        scratch_shapes=[pltpu.VMEM(w.shape, BF16) for w in flat]
        + [pltpu.VMEM((n_tiles * 4, 2 * half), BF16)] * 3
        + [pltpu.VMEM((n_tiles * 4, 2 * half), F32), pltpu.SemaphoreType.DMA((len(flat),))],
        compiler_params=pltpu.CompilerParams(vmem_limit_bytes=56 << 20),
        name="expert",
    )(rows, *flat)
    return out.reshape(n_tiles, 8, half)


def combine_kernel(ids_ref, slots_ref, gain_ref, scale_ref, layer_ref, back_ref, out_ref):
    enc_len, width = layer_ref.shape
    half = width // 2
    row = column_of((ids_ref[...] * 8 + slots_ref[...]).astype(F32)).astype(jnp.int32)
    at = lax.broadcasted_iota(jnp.int32, (enc_len, back_ref.shape[0]), 1)
    row_scale = gain_ref[...] * scale_ref[:, :1]
    for i in range(2):
        lanes = slice(i * half, (i + 1) * half)
        chosen = jnp.where(at == row + 4 * i, 1.0, 0.0).astype(BF16)
        per_token = mm(chosen, back_ref[...])
        out_ref[:, lanes] = (layer_ref[:, lanes] + row_scale[:, lanes] * per_token).astype(BF16)


def combine(ids, slots, gain, scale, layer_mult, back):
    return pl.pallas_call(
        combine_kernel,
        in_specs=[pl.BlockSpec(memory_space=pltpu.VMEM)] * 6,
        out_specs=pl.BlockSpec(memory_space=pltpu.VMEM),
        out_shape=jax.ShapeDtypeStruct(layer_mult.shape, BF16),
        compiler_params=pltpu.CompilerParams(vmem_limit_bytes=32 << 20),
        name="combine",
    )(ids, slots, gain, scale, layer_mult, back)


def exchange_weights(w_in, w_out_t, n_expert_devices):
    axes = ("expert", "dp")
    dp_at = lax.axis_index("dp")
    pieces = []
    for step in range(2):
        pairs = []
        for chip in range(n_expert_devices // 2):
            for core in range(2):
                for part in range(4):
                    own = (part // 2 + step) % 2
                    to_dp, to_core = 2 * core + own, part % 2
                    pairs.append(((chip * 2 + core) * 4 + part, (chip * 2 + to_core) * 4 + to_dp))
        own = (dp_at // 2 + step) % 2
        for weights in (w_in, w_out_t):
            sent = lax.dynamic_index_in_dim(weights, own, 0, keepdims=False)
            pieces.append(lax.ppermute(sent, axes, pairs))
    swap = [(i, i ^ 1) for i in range(n_expert_devices)]
    swapped = [lax.ppermute(piece, "expert", swap) for piece in pieces]
    both = pieces + swapped
    return list(zip(both[0::2], both[1::2]))


def body(
    enc_state, baseline, enc_keys, dec_queries, out_mult, doc_lengths, expert_ids, slot_ids, gate_prob, norm_gain,
    w_in, w_out_t, w_value,
):
    enc_len, width = enc_state.shape[2:]
    n_expert_devices = lax.axis_size("expert")
    n_experts = w_in.shape[0] * n_expert_devices
    axes = ("expert", "dp")
    groups = [
        [(chip * 2 + core) * 4 + at for chip in range(n_expert_devices // 2) for at in range(4)] for core in range(2)
    ]

    def exchange(rows):
        return lax.all_to_all(rows, axes, split_axis=0, concat_axis=0, axis_index_groups=groups, tiled=True)

    parts = exchange_weights(w_in, w_out_t, n_expert_devices)
    ids, slots, gain = expert_ids[0], slot_ids[0], norm_gain[None, :]
    placed, layer_mult, scale = prepare(
        doc_lengths, ids, slots, gate_prob[0], gain, enc_state[0, 0], baseline[0, 0], enc_keys[0, 0],
        dec_queries[0, 0], out_mult[0, 0], w_value, n_experts * 8,
    )
    came = exchange(placed.reshape(n_experts, 8, 3 * width // 2))
    slot_mult = expert_terms(came, parts)
    back = exchange(slot_mult)
    result = combine(ids, slots, gain, scale, layer_mult, back.reshape(n_experts * 8, width // 2))
    return result[None, None]


def solution(mesh):
    rows = P("dp", "expert", None)
    in_specs = (P("dp", "expert", None, None),) * 5 + (P("dp", "expert"),) + (rows,) * 3 + (
        P(), P("expert", None, "dp"), P("expert", None, "dp"), P(),
    )
    out_specs = P("dp", "expert", None, None)
    return jax.shard_map(body, mesh=mesh, in_specs=in_specs, out_specs=out_specs, check_vma=False)
```

```python
import math

import jax
import jax.numpy as jnp
from jax import lax
from jax.experimental import pallas as pl
from jax.experimental.pallas import tpu as pltpu
from jax.sharding import PartitionSpec as P

HEAD_DIM = 64
NT = (((1,), (1,)), ((), ()))
F32 = jnp.float32
BF16 = jnp.bfloat16


def mm(lhs, rhs):
    return jnp.dot(lhs, rhs, preferred_element_type=F32)


def mm_nt(lhs, rhs):
    return lax.dot_general(lhs, rhs, NT, preferred_element_type=F32)


def column_of(row):
    n = row.shape[1]
    eye = lax.broadcasted_iota(jnp.int32, (n, n), 0) == lax.broadcasted_iota(jnp.int32, (n, n), 1)
    return jnp.sum(jnp.where(eye, jnp.broadcast_to(row, (n, n)), 0.0), axis=1, keepdims=True)


def prepare_kernel(
    length_ref, ids_hbm, slots_hbm, gate_hbm, gain_hbm, enc_hbm, base_hbm, keys_hbm, query_hbm, mult_hbm, wv_hbm,
    placed_ref, layer_ref, scale_ref,
    ids_ref, slots_ref, gate_ref, gain_ref, enc_ref, base_ref, keys_ref, query_ref, mult_ref, wv_ref, value_ref, sems,
):
    enc_len, width = enc_ref.shape
    dec_len = query_ref.shape[0]
    copies = [
        pltpu.make_async_copy(src, dst, sems.at[i])
        for i, (src, dst) in enumerate(
            (
                (keys_hbm, keys_ref), (query_hbm, query_ref), (mult_hbm, mult_ref),
                (wv_hbm, wv_ref), (enc_hbm, enc_ref), (base_hbm, base_ref),
                (ids_hbm, ids_ref), (slots_hbm, slots_ref), (gate_hbm, gate_ref), (gain_hbm, gain_ref),
            )
        )
    ]
    for copy in copies:
        copy.start()
    for copy in copies[:3]:
        copy.wait()
    first = lax.broadcasted_iota(jnp.int32, (dec_len, 2 * HEAD_DIM), 1) < HEAD_DIM
    valid = lax.broadcasted_iota(jnp.int32, (enc_len, 2 * dec_len), 0) < length_ref[0, 0]
    for pair in range(width // (2 * HEAD_DIM)):
        lanes = slice(pair * 2 * HEAD_DIM, (pair + 1) * 2 * HEAD_DIM)
        query, mult = query_ref[:, lanes], mult_ref[:, lanes]
        zeros = jnp.zeros_like(query)
        queries = jnp.concatenate([jnp.where(first, query, zeros), jnp.where(first, zeros, query)], axis=0)
        mults = jnp.concatenate([jnp.where(first, mult, zeros), jnp.where(first, zeros, mult)], axis=0)
        scores = mm_nt(keys_ref[:, lanes], queries) * (1.0 / math.sqrt(HEAD_DIM))
        scores = jnp.where(valid, scores, -jnp.inf)
        expo = jnp.exp(scores - jnp.max(scores, axis=0, keepdims=True))
        attn = (expo * (1.0 / jnp.sum(expo, axis=0, keepdims=True))).astype(BF16)
        value_ref[:, lanes] = mm(attn, mults).astype(BF16)
    copies[3].wait()
    for copy in copies[6:]:
        copy.wait()
    layer_mult = mm_nt(value_ref[...], wv_ref[...])
    layer_ref[...] = layer_mult
    scaled_mult = (column_of(gate_ref[...]) * layer_mult).astype(BF16)
    copies[4].wait()
    copies[5].wait()
    tokens = enc_ref[...].astype(F32)
    inv = lax.rsqrt(jnp.mean(tokens * tokens, axis=-1, keepdims=True) + 1e-06)
    scale_ref[...] = jnp.broadcast_to(inv, scale_ref.shape)
    row_scale = gain_ref[...] * inv
    inputs = (tokens * row_scale).astype(BF16)
    base_inputs = (base_ref[...].astype(F32) * row_scale).astype(BF16)
    half = width // 2
    row = ids_ref[...] * 8 + slots_ref[...]
    at = lax.broadcasted_iota(jnp.int32, (placed_ref.shape[0], enc_len), 0)
    low = jnp.where(at == row, 1.0, 0.0).astype(BF16)
    high = jnp.where(at == row + 4, 1.0, 0.0).astype(BF16)
    placed_ref[:, :half] = (mm(low, inputs[:, :half]) + mm(high, inputs[:, half:])).astype(BF16)
    placed_ref[:, half:width] = (mm(low, base_inputs[:, :half]) + mm(high, base_inputs[:, half:])).astype(BF16)
    placed_ref[:, width:] = (mm(low, scaled_mult[:, :half]) + mm(high, scaled_mult[:, half:])).astype(BF16)


def prepare(length, ids, slots, gate, gain, enc, base, keys, query, mult, wv, n_rows):
    enc_len, width = enc.shape
    vmem = pl.BlockSpec(memory_space=pltpu.VMEM)
    taken = (ids, slots, gate, gain, enc, base, keys, query, mult, wv)
    return pl.pallas_call(
        prepare_kernel,
        in_specs=[pl.BlockSpec(memory_space=pltpu.SMEM)] + [pl.BlockSpec(memory_space=pltpu.HBM)] * len(taken),
        out_specs=[vmem] * 3,
        out_shape=[
            jax.ShapeDtypeStruct((n_rows, 3 * width // 2), BF16),
            jax.ShapeDtypeStruct((enc_len, width), F32),
            jax.ShapeDtypeStruct((enc_len, 128), F32),
        ],
        scratch_shapes=[pltpu.VMEM(a.shape, a.dtype) for a in taken]
        + [pltpu.VMEM((enc_len, width), BF16), pltpu.SemaphoreType.DMA((len(taken),))],
        compiler_params=pltpu.CompilerParams(vmem_limit_bytes=62 << 20),
        name="prepare",
    )(length, *taken)


def expert_kernel(rows_ref, *refs, n_parts):
    bundles_hbm = refs[:n_parts]
    out_ref, in_ref, mult_ref, w_in_ref, w_out_ref, act_ref, sems = refs[n_parts:]
    part_len = bundles_hbm[0].shape[0] // 2
    copies = [
        pltpu.make_async_copy(
            bundles_hbm[part].at[pl.ds(which * part_len, part_len)],
            ref.at[pl.ds(part * part_len, part_len)],
            sems.at[2 * part + which],
        )
        for part in range(n_parts)
        for which, ref in enumerate((w_in_ref, w_out_ref))
    ]
    for copy in copies:
        copy.start()
    n_tiles, _, lanes = rows_ref.shape
    half = lanes // 3
    n_rows = n_tiles * 4
    upper_rows = lax.broadcasted_iota(jnp.int32, (n_tiles // 2, 8, half), 1) < 4
    for i, ref in enumerate((in_ref.at[:n_rows], in_ref.at[n_rows:], mult_ref)):
        block = rows_ref[:, :, i * half : (i + 1) * half].astype(F32).reshape(n_tiles // 2, 2, 8, half)
        even, odd = block[:, 0], block[:, 1]
        low = jnp.where(upper_rows, even, pltpu.roll(odd, 4, 1))
        high = jnp.where(upper_rows, pltpu.roll(even, 4, 1), odd)
        ref[:, :half] = low.reshape(n_rows, half).astype(BF16)
        ref[:, half:] = high.reshape(n_rows, half).astype(BF16)
    hidden = n_parts * part_len
    block = 256
    waited = 0
    for at in range(0, hidden, block):
        cols = slice(at, at + block)
        while waited < 2 * n_parts and waited // 2 * part_len < at + block:
            copies[waited].wait()
            waited += 1
        both = mm_nt(in_ref[...], w_in_ref[cols, :])
        pre_act, base_act = both[:n_rows], both[n_rows:]
        hidden_mult = mm_nt(mult_ref[...], w_out_ref[cols, :])
        upper_part = jnp.maximum(jnp.maximum(pre_act, base_act), 0.0)
        lower_part = jnp.maximum(-jnp.minimum(pre_act, base_act), 0.0)
        ratio = upper_part / (upper_part + lower_part + jnp.where(upper_part > 0.0, 0.0, 1.0))
        act_ref[:, cols] = (ratio * hidden_mult).astype(BF16)
    low = mm(act_ref[...], w_in_ref[:, :half]).reshape(n_tiles // 2, 8, half)
    high = mm(act_ref[...], w_in_ref[:, half:]).reshape(n_tiles // 2, 8, half)
    out_ref[:, 0] = jnp.where(upper_rows, low, pltpu.roll(high, 4, 1)).astype(BF16)
    out_ref[:, 1] = jnp.where(upper_rows, pltpu.roll(low, 4, 1), high).astype(BF16)


def expert_terms(rows, parts):
    n_tiles, _, lanes = rows.shape
    half = lanes // 3
    n_rows, width = n_tiles * 4, 2 * half
    hidden = len(parts) * (parts[0].shape[0] // 2)
    out = pl.pallas_call(
        lambda *refs: expert_kernel(*refs, n_parts=len(parts)),
        in_specs=[pl.BlockSpec(memory_space=pltpu.VMEM)] + [pl.BlockSpec(memory_space=pltpu.HBM)] * len(parts),
        out_specs=pl.BlockSpec(memory_space=pltpu.VMEM),
        out_shape=jax.ShapeDtypeStruct((n_tiles // 2, 2, 8, half), BF16),
        scratch_shapes=[
            pltpu.VMEM((2 * n_rows, width), BF16), pltpu.VMEM((n_rows, width), BF16),
            pltpu.VMEM((hidden, width), BF16), pltpu.VMEM((hidden, width), BF16),
            pltpu.VMEM((n_rows, hidden), BF16), pltpu.SemaphoreType.DMA((2 * len(parts),)),
        ],
        compiler_params=pltpu.CompilerParams(vmem_limit_bytes=62 << 20),
        name="expert",
    )(rows, *parts)
    return out.reshape(n_tiles, 8, half)


def combine_kernel(ids_ref, slots_ref, gain_ref, scale_ref, layer_ref, back_ref, out_ref):
    enc_len, width = layer_ref.shape
    half = width // 2
    row = column_of((ids_ref[...] * 8 + slots_ref[...]).astype(F32)).astype(jnp.int32)
    at = lax.broadcasted_iota(jnp.int32, (enc_len, back_ref.shape[0]), 1)
    row_scale = gain_ref[...] * scale_ref[:, :1]
    for i in range(2):
        lanes = slice(i * half, (i + 1) * half)
        chosen = jnp.where(at == row + 4 * i, 1.0, 0.0).astype(BF16)
        per_token = mm(chosen, back_ref[...])
        out_ref[:, lanes] = (layer_ref[:, lanes] + row_scale[:, lanes] * per_token).astype(BF16)


def combine(ids, slots, gain, scale, layer_mult, back):
    return pl.pallas_call(
        combine_kernel,
        in_specs=[pl.BlockSpec(memory_space=pltpu.VMEM)] * 6,
        out_specs=pl.BlockSpec(memory_space=pltpu.VMEM),
        out_shape=jax.ShapeDtypeStruct(layer_mult.shape, BF16),
        compiler_params=pltpu.CompilerParams(vmem_limit_bytes=32 << 20),
        name="combine",
    )(ids, slots, gain, scale, layer_mult, back)


def exchange_weights(w_in, w_out_t, n_expert_devices):
    axes = ("expert", "dp")
    first_round, second_round = [], []
    for chip in range(n_expert_devices // 2):
        for core in range(2):
            for at in range(4):
                home = at // 2
                here = (chip * 2 + core) * 4 + at
                if core == home:
                    first_to, first_core = at ^ 1, 1 - home
                    second_to, second_core = at ^ 1, home
                else:
                    first_to, first_core = 3 - at, core
                    second_to, second_core = 3 - at, 1 - core
                first_round.append((here, (chip * 2 + first_core) * 4 + first_to))
                second_round.append((here, (chip * 2 + second_core) * 4 + second_to))
    at = lax.axis_index("dp")
    is_home = (at // 2) == (lax.axis_index("expert") % 2)
    first = jnp.where(is_home, 1 - at % 2, at % 2)
    w_in, w_out_t = jnp.swapaxes(w_in, 1, 2), jnp.swapaxes(w_out_t, 1, 2)

    def bundle(own):
        return jnp.concatenate(
            [lax.dynamic_index_in_dim(w, own, 0, keepdims=False) for w in (w_in, w_out_t)], axis=0
        )

    came = lax.ppermute(bundle(first), axes, first_round)
    rest = bundle(1 - first)
    kept = jnp.where(is_home, rest, came)
    onward = jnp.where(is_home, came, rest)
    swap = [(i, i ^ 1) for i in range(n_expert_devices)]
    last = lax.ppermute(onward, axes, second_round)
    return [kept, lax.ppermute(kept, "expert", swap), last, lax.ppermute(last, "expert", swap)]


def body(
    enc_state, baseline, enc_keys, dec_queries, out_mult, doc_lengths, expert_ids, slot_ids, gate_prob, norm_gain,
    w_in, w_out_t, w_value,
):
    enc_len, width = enc_state.shape[2:]
    n_expert_devices = lax.axis_size("expert")
    n_experts = w_in.shape[0] * n_expert_devices
    axes = ("expert", "dp")
    groups = [
        [(chip * 2 + core) * 4 + at for chip in range(n_expert_devices // 2) for at in range(4)] for core in range(2)
    ]

    def exchange(rows):
        return lax.all_to_all(rows, axes, split_axis=0, concat_axis=0, axis_index_groups=groups, tiled=True)

    parts = exchange_weights(w_in, w_out_t, n_expert_devices)
    ids, slots, gain = expert_ids[0], slot_ids[0], norm_gain[None, :]
    placed, layer_mult, scale = prepare(
        doc_lengths, ids, slots, gate_prob[0], gain, enc_state[0, 0], baseline[0, 0], enc_keys[0, 0],
        dec_queries[0, 0], out_mult[0, 0], w_value, n_experts * 8,
    )
    came = exchange(placed.reshape(n_experts, 8, 3 * width // 2))
    slot_mult = expert_terms(came, parts)
    back = exchange(slot_mult)
    result = combine(ids, slots, gain, scale, layer_mult, back.reshape(n_experts * 8, width // 2))
    return result[None, None]


def solution(mesh):
    rows = P("dp", "expert", None)
    in_specs = (P("dp", "expert", None, None),) * 5 + (P("dp", "expert"),) + (rows,) * 3 + (
        P(), P("expert", None, "dp"), P("expert", None, "dp"), P(),
    )
    out_specs = P("dp", "expert", None, None)
    return jax.shard_map(body, mesh=mesh, in_specs=in_specs, out_specs=out_specs, check_vma=False)
```

```python
import math

import jax
import jax.numpy as jnp
from jax import lax
from jax.experimental import pallas as pl
from jax.experimental.pallas import tpu as pltpu
from jax.sharding import PartitionSpec as P

HEAD_DIM = 64
NT = (((1,), (1,)), ((), ()))
F32 = jnp.float32
BF16 = jnp.bfloat16


def mm(lhs, rhs):
    return jnp.dot(lhs, rhs, preferred_element_type=F32)


def mm_nt(lhs, rhs):
    return lax.dot_general(lhs, rhs, NT, preferred_element_type=F32)


def column_of(row):
    n = row.shape[1]
    eye = lax.broadcasted_iota(jnp.int32, (n, n), 0) == lax.broadcasted_iota(jnp.int32, (n, n), 1)
    return jnp.sum(jnp.where(eye, jnp.broadcast_to(row, (n, n)), 0.0), axis=1, keepdims=True)


def prepare_kernel(
    length_ref, ids_hbm, slots_hbm, gate_hbm, gain_hbm, enc_hbm, base_hbm, keys_hbm, query_hbm, mult_hbm, wv_hbm,
    placed_ref, layer_ref, scale_ref,
    ids_ref, slots_ref, gate_ref, gain_ref, enc_ref, base_ref, keys_ref, query_ref, mult_ref, wv_ref, value_ref, sems,
):
    enc_len, width = enc_ref.shape
    dec_len = query_ref.shape[0]
    copies = [
        pltpu.make_async_copy(src, dst, sems.at[i])
        for i, (src, dst) in enumerate(
            (
                (keys_hbm, keys_ref), (query_hbm, query_ref), (mult_hbm, mult_ref),
                (wv_hbm, wv_ref), (enc_hbm, enc_ref), (base_hbm, base_ref),
                (ids_hbm, ids_ref), (slots_hbm, slots_ref), (gate_hbm, gate_ref), (gain_hbm, gain_ref),
            )
        )
    ]
    for copy in copies:
        copy.start()
    for copy in copies[:3]:
        copy.wait()
    first = lax.broadcasted_iota(jnp.int32, (dec_len, 2 * HEAD_DIM), 1) < HEAD_DIM
    valid = lax.broadcasted_iota(jnp.int32, (enc_len, 2 * dec_len), 0) < length_ref[0, 0]
    for pair in range(width // (2 * HEAD_DIM)):
        lanes = slice(pair * 2 * HEAD_DIM, (pair + 1) * 2 * HEAD_DIM)
        query, mult = query_ref[:, lanes], mult_ref[:, lanes]
        zeros = jnp.zeros_like(query)
        queries = jnp.concatenate([jnp.where(first, query, zeros), jnp.where(first, zeros, query)], axis=0)
        mults = jnp.concatenate([jnp.where(first, mult, zeros), jnp.where(first, zeros, mult)], axis=0)
        scores = mm_nt(keys_ref[:, lanes], queries) * (1.0 / math.sqrt(HEAD_DIM))
        scores = jnp.where(valid, scores, -jnp.inf)
        expo = jnp.exp(scores - jnp.max(scores, axis=0, keepdims=True))
        attn = (expo * (1.0 / jnp.sum(expo, axis=0, keepdims=True))).astype(BF16)
        value_ref[:, lanes] = mm(attn, mults).astype(BF16)
    copies[3].wait()
    for copy in copies[6:]:
        copy.wait()
    layer_mult = mm_nt(value_ref[...], wv_ref[...])
    layer_ref[...] = layer_mult
    scaled_mult = (column_of(gate_ref[...]) * layer_mult).astype(BF16)
    copies[4].wait()
    copies[5].wait()
    tokens = enc_ref[...].astype(F32)
    inv = lax.rsqrt(jnp.mean(tokens * tokens, axis=-1, keepdims=True) + 1e-06)
    scale_ref[...] = jnp.broadcast_to(inv, scale_ref.shape)
    row_scale = gain_ref[...] * inv
    inputs = (tokens * row_scale).astype(BF16)
    base_inputs = (base_ref[...].astype(F32) * row_scale).astype(BF16)
    half = width // 2
    row = ids_ref[...] * 8 + slots_ref[...]
    at = lax.broadcasted_iota(jnp.int32, (placed_ref.shape[0], enc_len), 0)
    low = jnp.where(at == row, 1.0, 0.0).astype(BF16)
    high = jnp.where(at == row + 4, 1.0, 0.0).astype(BF16)
    placed_ref[:, :half] = (mm(low, inputs[:, :half]) + mm(high, inputs[:, half:])).astype(BF16)
    placed_ref[:, half:width] = (mm(low, base_inputs[:, :half]) + mm(high, base_inputs[:, half:])).astype(BF16)
    placed_ref[:, width:] = (mm(low, scaled_mult[:, :half]) + mm(high, scaled_mult[:, half:])).astype(BF16)


def prepare(length, ids, slots, gate, gain, enc, base, keys, query, mult, wv, n_rows):
    enc_len, width = enc.shape
    vmem = pl.BlockSpec(memory_space=pltpu.VMEM)
    taken = (ids, slots, gate, gain, enc, base, keys, query, mult, wv)
    return pl.pallas_call(
        prepare_kernel,
        in_specs=[pl.BlockSpec(memory_space=pltpu.SMEM)] + [pl.BlockSpec(memory_space=pltpu.HBM)] * len(taken),
        out_specs=[vmem] * 3,
        out_shape=[
            jax.ShapeDtypeStruct((n_rows, 3 * width // 2), BF16),
            jax.ShapeDtypeStruct((enc_len, width), F32),
            jax.ShapeDtypeStruct((enc_len, 128), F32),
        ],
        scratch_shapes=[pltpu.VMEM(a.shape, a.dtype) for a in taken]
        + [pltpu.VMEM((enc_len, width), BF16), pltpu.SemaphoreType.DMA((len(taken),))],
        compiler_params=pltpu.CompilerParams(vmem_limit_bytes=62 << 20),
        name="prepare",
    )(length, *taken)


def expert_kernel(rows_hbm, *refs, n_parts):
    weights_hbm = refs[: 2 * n_parts]
    out_ref, rows_ref, in_ref, mult_ref, w_in_ref, w_out_ref, act_ref, sems = refs[2 * n_parts :]
    n_tiles, _, lanes = rows_ref.shape
    half = lanes // 3
    n_rows = n_tiles * 4
    part_len = weights_hbm[0].shape[0]
    copies = [
        pltpu.make_async_copy(
            weights_hbm[i], (w_in_ref, w_out_ref)[i % 2].at[pl.ds(i // 2 * part_len, part_len)], sems.at[i]
        )
        for i in range(2 * n_parts)
    ]
    row_copies = []
    for i in range(3):
        lanes_of = (slice(None), slice(None), pl.ds(i * half, half))
        row_copies.append(
            pltpu.make_async_copy(rows_hbm.at[lanes_of], rows_ref.at[lanes_of], sems.at[2 * n_parts + i])
        )
    for copy in [*row_copies[:2], copies[0], row_copies[2], *copies[1:]]:
        copy.start()
    upper_rows = lax.broadcasted_iota(jnp.int32, (n_tiles // 2, 8, half), 1) < 4
    for i, ref in enumerate((in_ref.at[:n_rows], in_ref.at[n_rows:], mult_ref)):
        row_copies[i].wait()
        block = rows_ref[:, :, i * half : (i + 1) * half].astype(F32).reshape(n_tiles // 2, 2, 8, half)
        even, odd = block[:, 0], block[:, 1]
        low = jnp.where(upper_rows, even, pltpu.roll(odd, 4, 1))
        high = jnp.where(upper_rows, pltpu.roll(even, 4, 1), odd)
        ref[:, :half] = low.reshape(n_rows, half).astype(BF16)
        ref[:, half:] = high.reshape(n_rows, half).astype(BF16)
    hidden = n_parts * part_len
    block = 256
    waited = 0
    for at in range(0, hidden, block):
        cols = slice(at, at + block)
        while waited < 2 * n_parts and waited // 2 * part_len < at + block:
            copies[waited].wait()
            waited += 1
        both = mm_nt(in_ref[...], w_in_ref[cols, :])
        pre_act, base_act = both[:n_rows], both[n_rows:]
        hidden_mult = mm_nt(mult_ref[...], w_out_ref[cols, :])
        upper_part = jnp.maximum(jnp.maximum(pre_act, base_act), 0.0)
        lower_part = jnp.maximum(-jnp.minimum(pre_act, base_act), 0.0)
        ratio = upper_part / (upper_part + lower_part + jnp.where(upper_part > 0.0, 0.0, 1.0))
        act_ref[:, cols] = (ratio * hidden_mult).astype(BF16)
    low = mm(act_ref[...], w_in_ref[:, :half]).reshape(n_tiles // 2, 8, half)
    high = mm(act_ref[...], w_in_ref[:, half:]).reshape(n_tiles // 2, 8, half)
    out_ref[:, 0] = jnp.where(upper_rows, low, pltpu.roll(high, 4, 1)).astype(BF16)
    out_ref[:, 1] = jnp.where(upper_rows, pltpu.roll(low, 4, 1), high).astype(BF16)


def expert_terms(rows, parts):
    n_tiles, _, lanes = rows.shape
    half = lanes // 3
    n_rows, width = n_tiles * 4, 2 * half
    n_parts = len(parts) // 2
    hidden = n_parts * parts[0].shape[0]
    out = pl.pallas_call(
        lambda *refs: expert_kernel(*refs, n_parts=n_parts),
        in_specs=[pl.BlockSpec(memory_space=pltpu.HBM)] * (1 + len(parts)),
        out_specs=pl.BlockSpec(memory_space=pltpu.VMEM),
        out_shape=jax.ShapeDtypeStruct((n_tiles // 2, 2, 8, half), BF16),
        scratch_shapes=[
            pltpu.VMEM(rows.shape, BF16), pltpu.VMEM((2 * n_rows, width), BF16), pltpu.VMEM((n_rows, width), BF16),
            pltpu.VMEM((hidden, width), BF16), pltpu.VMEM((hidden, width), BF16),
            pltpu.VMEM((n_rows, hidden), BF16), pltpu.SemaphoreType.DMA((len(parts) + 3,)),
        ],
        compiler_params=pltpu.CompilerParams(vmem_limit_bytes=62 << 20),
        name="expert",
    )(rows, *parts)
    return out.reshape(n_tiles, 8, half)


def combine_kernel(ids_ref, slots_ref, gain_ref, scale_ref, layer_ref, back_ref, out_ref):
    enc_len, width = layer_ref.shape
    half = width // 2
    row = column_of((ids_ref[...] * 8 + slots_ref[...]).astype(F32)).astype(jnp.int32)
    at = lax.broadcasted_iota(jnp.int32, (enc_len, back_ref.shape[0]), 1)
    row_scale = gain_ref[...] * scale_ref[:, :1]
    for i in range(2):
        lanes = slice(i * half, (i + 1) * half)
        chosen = jnp.where(at == row + 4 * i, 1.0, 0.0).astype(BF16)
        per_token = mm(chosen, back_ref[...])
        out_ref[:, lanes] = (layer_ref[:, lanes] + row_scale[:, lanes] * per_token).astype(BF16)


def combine(ids, slots, gain, scale, layer_mult, back):
    return pl.pallas_call(
        combine_kernel,
        in_specs=[pl.BlockSpec(memory_space=pltpu.VMEM)] * 6,
        out_specs=pl.BlockSpec(memory_space=pltpu.VMEM),
        out_shape=jax.ShapeDtypeStruct(layer_mult.shape, BF16),
        compiler_params=pltpu.CompilerParams(vmem_limit_bytes=32 << 20),
        name="combine",
    )(ids, slots, gain, scale, layer_mult, back)


def exchange_weights(w_in, w_out_t, rows, n_expert_devices):
    axes = ("expert", "dp")
    first_round, second_round = [], []
    for chip in range(n_expert_devices // 2):
        for core in range(2):
            for at in range(4):
                home = at // 2
                here = (chip * 2 + core) * 4 + at
                if core == home:
                    first_to, first_core = at ^ 1, 1 - home
                    second_to, second_core = at ^ 1, home
                else:
                    first_to, first_core = 3 - at, core
                    second_to, second_core = 3 - at, 1 - core
                first_round.append((here, (chip * 2 + first_core) * 4 + first_to))
                second_round.append((here, (chip * 2 + second_core) * 4 + second_to))
    at = lax.axis_index("dp")
    is_home = (at // 2) == (lax.axis_index("expert") % 2)
    first = jnp.where(is_home, 1 - at % 2, at % 2)
    w_in, w_out_t = jnp.swapaxes(w_in, 1, 2), jnp.swapaxes(w_out_t, 1, 2)

    swap = [(i, i ^ 1) for i in range(n_expert_devices)]
    kept, last = [], []
    for weights in (w_in, w_out_t):
        came = lax.ppermute(lax.dynamic_index_in_dim(weights, first, 0, keepdims=False), axes, first_round)
        came, late = lax.optimization_barrier((came, weights))
        rest = lax.dynamic_index_in_dim(late, 1 - first, 0, keepdims=False)
        kept.append(jnp.where(is_home, rest, came))
        last.append(lax.ppermute(jnp.where(is_home, came, rest), axes, second_round))
    kept = lax.optimization_barrier(kept)
    other = []
    for i, piece in enumerate(kept + last):
        if other:
            other[-1], piece = lax.optimization_barrier((other[-1], piece))
        if i == 3:
            rows, piece = lax.optimization_barrier((rows, piece))
        other.append(lax.ppermute(piece, "expert", swap))
    return rows, kept + last + other


def body(
    enc_state, baseline, enc_keys, dec_queries, out_mult, doc_lengths, expert_ids, slot_ids, gate_prob, norm_gain,
    w_in, w_out_t, w_value,
):
    enc_len, width = enc_state.shape[2:]
    n_expert_devices = lax.axis_size("expert")
    n_experts = w_in.shape[0] * n_expert_devices
    axes = ("expert", "dp")
    groups = [
        [(chip * 2 + core) * 4 + at for chip in range(n_expert_devices // 2) for at in range(4)] for core in range(2)
    ]

    def exchange(rows):
        return lax.all_to_all(rows, axes, split_axis=0, concat_axis=0, axis_index_groups=groups, tiled=True)

    ids, slots, gain = expert_ids[0], slot_ids[0], norm_gain[None, :]
    placed, layer_mult, scale = prepare(
        doc_lengths, ids, slots, gate_prob[0], gain, enc_state[0, 0], baseline[0, 0], enc_keys[0, 0],
        dec_queries[0, 0], out_mult[0, 0], w_value, n_experts * 8,
    )
    came = exchange(placed.reshape(n_experts, 8, 3 * width // 2))
    came, parts = exchange_weights(w_in, w_out_t, came, n_expert_devices)
    slot_mult = expert_terms(came, parts)
    back = exchange(slot_mult)
    result = combine(ids, slots, gain, scale, layer_mult, back.reshape(n_experts * 8, width // 2))
    return result[None, None]


def solution(mesh):
    rows = P("dp", "expert", None)
    in_specs = (P("dp", "expert", None, None),) * 5 + (P("dp", "expert"),) + (rows,) * 3 + (
        P(), P("expert", None, "dp"), P("expert", None, "dp"), P(),
    )
    out_specs = P("dp", "expert", None, None)
    return jax.shard_map(body, mesh=mesh, in_specs=in_specs, out_specs=out_specs, check_vma=False)
```

```python
import math

import jax
import jax.numpy as jnp
from jax import lax
from jax.experimental import pallas as pl
from jax.experimental.pallas import tpu as pltpu
from jax.sharding import PartitionSpec as P

HEAD_DIM = 64
NT = (((1,), (1,)), ((), ()))
F32 = jnp.float32
BF16 = jnp.bfloat16


def mm(lhs, rhs):
    return jnp.dot(lhs, rhs, preferred_element_type=F32)


def mm_nt(lhs, rhs):
    return lax.dot_general(lhs, rhs, NT, preferred_element_type=F32)


def column_of(row):
    n = row.shape[1]
    eye = lax.broadcasted_iota(jnp.int32, (n, n), 0) == lax.broadcasted_iota(jnp.int32, (n, n), 1)
    return jnp.sum(jnp.where(eye, jnp.broadcast_to(row, (n, n)), 0.0), axis=1, keepdims=True)


def prepare_kernel(
    length_ref, ids_hbm, slots_hbm, gate_hbm, gain_hbm, enc_hbm, base_hbm, keys_hbm, query_hbm, mult_hbm, wv_hbm,
    placed_ref, layer_ref, scale_ref,
    ids_ref, slots_ref, gate_ref, gain_ref, enc_ref, base_ref, keys_ref, query_ref, mult_ref, wv_ref, value_ref, sems,
):
    enc_len, width = enc_ref.shape
    dec_len = query_ref.shape[0]
    copies = [
        pltpu.make_async_copy(src, dst, sems.at[i])
        for i, (src, dst) in enumerate(
            (
                (keys_hbm, keys_ref), (query_hbm, query_ref), (mult_hbm, mult_ref),
                (wv_hbm, wv_ref), (enc_hbm, enc_ref), (base_hbm, base_ref),
                (ids_hbm, ids_ref), (slots_hbm, slots_ref), (gate_hbm, gate_ref), (gain_hbm, gain_ref),
            )
        )
    ]
    for copy in copies:
        copy.start()
    for copy in copies[:3]:
        copy.wait()
    first = lax.broadcasted_iota(jnp.int32, (dec_len, 2 * HEAD_DIM), 1) < HEAD_DIM
    valid = lax.broadcasted_iota(jnp.int32, (enc_len, 2 * dec_len), 0) < length_ref[0, 0]
    for pair in range(width // (2 * HEAD_DIM)):
        lanes = slice(pair * 2 * HEAD_DIM, (pair + 1) * 2 * HEAD_DIM)
        query, mult = query_ref[:, lanes], mult_ref[:, lanes]
        zeros = jnp.zeros_like(query)
        queries = jnp.concatenate([jnp.where(first, query, zeros), jnp.where(first, zeros, query)], axis=0)
        mults = jnp.concatenate([jnp.where(first, mult, zeros), jnp.where(first, zeros, mult)], axis=0)
        scores = mm_nt(keys_ref[:, lanes], queries) * (1.0 / math.sqrt(HEAD_DIM))
        scores = jnp.where(valid, scores, -jnp.inf)
        expo = jnp.exp(scores - jnp.max(scores, axis=0, keepdims=True))
        attn = (expo * (1.0 / jnp.sum(expo, axis=0, keepdims=True))).astype(BF16)
        value_ref[:, lanes] = mm(attn, mults).astype(BF16)
    copies[3].wait()
    for copy in copies[6:]:
        copy.wait()
    layer_mult = mm_nt(value_ref[...], wv_ref[...])
    layer_ref[...] = layer_mult
    scaled_mult = (column_of(gate_ref[...]) * layer_mult).astype(BF16)
    copies[4].wait()
    copies[5].wait()
    tokens = enc_ref[...].astype(F32)
    inv = lax.rsqrt(jnp.mean(tokens * tokens, axis=-1, keepdims=True) + 1e-06)
    scale_ref[...] = jnp.broadcast_to(inv, scale_ref.shape)
    row_scale = gain_ref[...] * inv
    inputs = (tokens * row_scale).astype(BF16)
    base_inputs = (base_ref[...].astype(F32) * row_scale).astype(BF16)
    half = width // 2
    row = ids_ref[...] * 8 + slots_ref[...]
    at = lax.broadcasted_iota(jnp.int32, (placed_ref.shape[0], enc_len), 0)
    low = jnp.where(at == row, 1.0, 0.0).astype(BF16)
    high = jnp.where(at == row + 4, 1.0, 0.0).astype(BF16)
    placed_ref[:, :half] = (mm(low, inputs[:, :half]) + mm(high, inputs[:, half:])).astype(BF16)
    placed_ref[:, half:width] = (mm(low, base_inputs[:, :half]) + mm(high, base_inputs[:, half:])).astype(BF16)
    placed_ref[:, width:] = (mm(low, scaled_mult[:, :half]) + mm(high, scaled_mult[:, half:])).astype(BF16)


def prepare(length, ids, slots, gate, gain, enc, base, keys, query, mult, wv, n_rows):
    enc_len, width = enc.shape
    vmem = pl.BlockSpec(memory_space=pltpu.VMEM)
    taken = (ids, slots, gate, gain, enc, base, keys, query, mult, wv)
    return pl.pallas_call(
        prepare_kernel,
        in_specs=[pl.BlockSpec(memory_space=pltpu.SMEM)] + [pl.BlockSpec(memory_space=pltpu.HBM)] * len(taken),
        out_specs=[vmem] * 3,
        out_shape=[
            jax.ShapeDtypeStruct((n_rows, 3 * width // 2), BF16),
            jax.ShapeDtypeStruct((enc_len, width), F32),
            jax.ShapeDtypeStruct((enc_len, 128), F32),
        ],
        scratch_shapes=[pltpu.VMEM(a.shape, a.dtype) for a in taken]
        + [pltpu.VMEM((enc_len, width), BF16), pltpu.SemaphoreType.DMA((len(taken),))],
        compiler_params=pltpu.CompilerParams(vmem_limit_bytes=62 << 20),
        name="prepare",
    )(length, *taken)


def rescale(pre_act, base_act):
    upper_part = jnp.maximum(jnp.maximum(pre_act, base_act), 0.0)
    lower_part = jnp.maximum(-jnp.minimum(pre_act, base_act), 0.0)
    return upper_part / (upper_part + lower_part + jnp.where(upper_part > 0.0, 0.0, 1.0))


def hidden_blocks(length, block=256):
    return [slice(at, min(at + block, length)) for at in range(0, length, block)]


def first_kernel(
    rows_hbm, kept_in, kept_in2, kept_out, kept_out2, last_in, last_in2,
    partial_ref, ratio_ref, mult_ref, rows_ref, in_ref, w_in_ref, w_out_ref, act_ref, sems,
):
    n_tiles, _, lanes = rows_ref.shape
    half = lanes // 3
    n_rows = n_tiles * 4
    part_len = kept_in.shape[0]
    hidden = 2 * part_len

    def part(src, dst, i, sem):
        return pltpu.make_async_copy(src, dst.at[pl.ds(i * part_len, part_len)], sems.at[sem])

    copies = [
        part(kept_in, w_in_ref, 0, 0), part(kept_out, w_out_ref, 0, 1), part(kept_in2, w_in_ref, 1, 2),
        part(kept_out2, w_out_ref, 1, 3), part(last_in, w_in_ref, 2, 4), part(last_in2, w_in_ref, 3, 5),
    ]
    row_copies = []
    for i in range(3):
        lanes_of = (slice(None), slice(None), pl.ds(i * half, half))
        row_copies.append(pltpu.make_async_copy(rows_hbm.at[lanes_of], rows_ref.at[lanes_of], sems.at[6 + i]))
    for copy in [*row_copies[:2], copies[0], row_copies[2], *copies[1:]]:
        copy.start()
    upper_rows = lax.broadcasted_iota(jnp.int32, (n_tiles // 2, 8, half), 1) < 4
    for i, ref in enumerate((in_ref.at[:n_rows], in_ref.at[n_rows:], mult_ref)):
        row_copies[i].wait()
        block = rows_ref[:, :, i * half : (i + 1) * half].astype(F32).reshape(n_tiles // 2, 2, 8, half)
        even, odd = block[:, 0], block[:, 1]
        low = jnp.where(upper_rows, even, pltpu.roll(odd, 4, 1))
        high = jnp.where(upper_rows, pltpu.roll(even, 4, 1), odd)
        ref[:, :half] = low.reshape(n_rows, half).astype(BF16)
        ref[:, half:] = high.reshape(n_rows, half).astype(BF16)
    for copy in copies[:2]:
        copy.wait()
    for i, cols in enumerate(hidden_blocks(hidden)):
        if i == part_len // 256:
            for copy in copies[2:4]:
                copy.wait()
        both = mm_nt(in_ref[...], w_in_ref[cols, :])
        hidden_mult = mm_nt(mult_ref[...], w_out_ref[cols, :])
        act_ref[:, cols] = (rescale(both[:n_rows], both[n_rows:]) * hidden_mult).astype(BF16)
    for copy in copies[4:]:
        copy.wait()
    for cols in hidden_blocks(hidden):
        both = mm_nt(in_ref[...], w_in_ref[slice(hidden + cols.start, hidden + cols.stop), :])
        ratio_ref[:, cols] = rescale(both[:n_rows], both[n_rows:])
    partial_ref[...] = mm(act_ref[...], w_in_ref[:hidden, :])


def last_kernel(
    mult_ref, partial_hbm, ratio_hbm, last_in, last_in2, last_out, last_out2,
    out_ref, partial_ref, ratio_ref, w_in_ref, w_out_ref, act_ref, sems,
):
    n_rows, width = mult_ref.shape
    half = width // 2
    n_tiles = n_rows // 4
    part_len = last_in.shape[0]
    hidden = 2 * part_len

    def part(src, dst, i, sem):
        return pltpu.make_async_copy(src, dst.at[pl.ds(i * part_len, part_len)], sems.at[sem])

    copies = [
        part(last_out, w_out_ref, 0, 0), pltpu.make_async_copy(ratio_hbm, ratio_ref, sems.at[1]),
        part(last_out2, w_out_ref, 1, 2), part(last_in, w_in_ref, 0, 3), part(last_in2, w_in_ref, 1, 4),
        pltpu.make_async_copy(partial_hbm, partial_ref, sems.at[5]),
    ]
    for copy in copies:
        copy.start()
    for copy in copies[:2]:
        copy.wait()
    for i, cols in enumerate(hidden_blocks(hidden)):
        if i == part_len // 256:
            copies[2].wait()
        act_ref[:, cols] = (ratio_ref[:, cols] * mm_nt(mult_ref[...], w_out_ref[cols, :])).astype(BF16)
    for copy in copies[3:]:
        copy.wait()
    upper_rows = lax.broadcasted_iota(jnp.int32, (n_tiles // 2, 8, half), 1) < 4
    low = (partial_ref[:, :half] + mm(act_ref[...], w_in_ref[:, :half])).reshape(n_tiles // 2, 8, half)
    high = (partial_ref[:, half:] + mm(act_ref[...], w_in_ref[:, half:])).reshape(n_tiles // 2, 8, half)
    out_ref[:, 0] = jnp.where(upper_rows, low, pltpu.roll(high, 4, 1)).astype(BF16)
    out_ref[:, 1] = jnp.where(upper_rows, pltpu.roll(low, 4, 1), high).astype(BF16)


def expert_first(rows, weights):
    n_tiles, _, lanes = rows.shape
    n_rows, width = n_tiles * 4, 2 * lanes // 3
    hidden = 2 * weights[0].shape[0]
    return pl.pallas_call(
        first_kernel,
        in_specs=[pl.BlockSpec(memory_space=pltpu.HBM)] * 7,
        out_specs=[pl.BlockSpec(memory_space=pltpu.VMEM)] * 3,
        out_shape=[
            jax.ShapeDtypeStruct((n_rows, width), F32), jax.ShapeDtypeStruct((n_rows, hidden), F32),
            jax.ShapeDtypeStruct((n_rows, width), BF16),
        ],
        scratch_shapes=[
            pltpu.VMEM(rows.shape, BF16), pltpu.VMEM((2 * n_rows, width), BF16),
            pltpu.VMEM((2 * hidden, width), BF16), pltpu.VMEM((hidden, width), BF16),
            pltpu.VMEM((n_rows, hidden), BF16), pltpu.SemaphoreType.DMA((9,)),
        ],
        compiler_params=pltpu.CompilerParams(vmem_limit_bytes=62 << 20),
        name="expert_first",
    )(rows, *weights)


def expert_last(mult, partial, ratio, weights):
    n_rows, width = mult.shape
    hidden = ratio.shape[1]
    return pl.pallas_call(
        last_kernel,
        in_specs=[pl.BlockSpec(memory_space=pltpu.VMEM)] + [pl.BlockSpec(memory_space=pltpu.HBM)] * 6,
        out_specs=pl.BlockSpec(memory_space=pltpu.VMEM),
        out_shape=jax.ShapeDtypeStruct((n_rows // 8, 2, 8, width // 2), BF16),
        scratch_shapes=[
            pltpu.VMEM((n_rows, width), F32), pltpu.VMEM((n_rows, hidden), F32),
            pltpu.VMEM((hidden, width), BF16), pltpu.VMEM((hidden, width), BF16),
            pltpu.VMEM((n_rows, hidden), BF16), pltpu.SemaphoreType.DMA((6,)),
        ],
        compiler_params=pltpu.CompilerParams(vmem_limit_bytes=62 << 20),
        name="expert_last",
    )(mult, partial, ratio, *weights)


def combine_kernel(ids_ref, slots_ref, gain_ref, scale_ref, layer_ref, back_ref, out_ref):
    enc_len, width = layer_ref.shape
    half = width // 2
    row = column_of((ids_ref[...] * 8 + slots_ref[...]).astype(F32)).astype(jnp.int32)
    at = lax.broadcasted_iota(jnp.int32, (enc_len, back_ref.shape[0]), 1)
    row_scale = gain_ref[...] * scale_ref[:, :1]
    for i in range(2):
        lanes = slice(i * half, (i + 1) * half)
        chosen = jnp.where(at == row + 4 * i, 1.0, 0.0).astype(BF16)
        per_token = mm(chosen, back_ref[...])
        out_ref[:, lanes] = (layer_ref[:, lanes] + row_scale[:, lanes] * per_token).astype(BF16)


def combine(ids, slots, gain, scale, layer_mult, back):
    return pl.pallas_call(
        combine_kernel,
        in_specs=[pl.BlockSpec(memory_space=pltpu.VMEM)] * 6,
        out_specs=pl.BlockSpec(memory_space=pltpu.VMEM),
        out_shape=jax.ShapeDtypeStruct(layer_mult.shape, BF16),
        compiler_params=pltpu.CompilerParams(vmem_limit_bytes=32 << 20),
        name="combine",
    )(ids, slots, gain, scale, layer_mult, back)


def expert_layer(w_in, w_out_t, rows, n_expert_devices):
    axes = ("expert", "dp")
    first_round, second_round = [], []
    for chip in range(n_expert_devices // 2):
        for core in range(2):
            for at in range(4):
                home = at // 2
                here = (chip * 2 + core) * 4 + at
                if core == home:
                    first_to, first_core = at ^ 1, 1 - home
                    second_to, second_core = at ^ 1, home
                else:
                    first_to, first_core = 3 - at, core
                    second_to, second_core = 3 - at, 1 - core
                first_round.append((here, (chip * 2 + first_core) * 4 + first_to))
                second_round.append((here, (chip * 2 + second_core) * 4 + second_to))
    at = lax.axis_index("dp")
    is_home = (at // 2) == (lax.axis_index("expert") % 2)
    first = jnp.where(is_home, 1 - at % 2, at % 2)
    w_in, w_out_t = jnp.swapaxes(w_in, 1, 2), jnp.swapaxes(w_out_t, 1, 2)

    swap = [(i, i ^ 1) for i in range(n_expert_devices)]
    kept, last = [], []
    for weights in (w_in, w_out_t):
        came = lax.ppermute(lax.dynamic_index_in_dim(weights, first, 0, keepdims=False), axes, first_round)
        came, late = lax.optimization_barrier((came, weights))
        rest = lax.dynamic_index_in_dim(late, 1 - first, 0, keepdims=False)
        kept.append(jnp.where(is_home, rest, came))
        last.append(lax.ppermute(jnp.where(is_home, came, rest), axes, second_round))
    kept = lax.optimization_barrier(kept)
    other = []
    for piece in [*kept, last[0]]:
        if other:
            other[-1], piece = lax.optimization_barrier((other[-1], piece))
        other.append(lax.ppermute(piece, "expert", swap))
    partial, ratio, mult = expert_first(rows, [kept[0], other[0], kept[1], other[1], last[0], other[2]])
    partial, final = lax.optimization_barrier((partial, last[1]))
    return expert_last(mult, partial, ratio, [last[0], other[2], final, lax.ppermute(final, "expert", swap)])


def body(
    enc_state, baseline, enc_keys, dec_queries, out_mult, doc_lengths, expert_ids, slot_ids, gate_prob, norm_gain,
    w_in, w_out_t, w_value,
):
    enc_len, width = enc_state.shape[2:]
    n_expert_devices = lax.axis_size("expert")
    n_experts = w_in.shape[0] * n_expert_devices
    axes = ("expert", "dp")
    groups = [
        [(chip * 2 + core) * 4 + at for chip in range(n_expert_devices // 2) for at in range(4)] for core in range(2)
    ]

    def exchange(rows):
        return lax.all_to_all(rows, axes, split_axis=0, concat_axis=0, axis_index_groups=groups, tiled=True)

    ids, slots, gain = expert_ids[0], slot_ids[0], norm_gain[None, :]
    placed, layer_mult, scale = prepare(
        doc_lengths, ids, slots, gate_prob[0], gain, enc_state[0, 0], baseline[0, 0], enc_keys[0, 0],
        dec_queries[0, 0], out_mult[0, 0], w_value, n_experts * 8,
    )
    came = exchange(placed.reshape(n_experts, 8, 3 * width // 2))
    slot_mult = expert_layer(w_in, w_out_t, came, n_expert_devices)
    back = exchange(slot_mult.reshape(n_experts, 8, width // 2))
    result = combine(ids, slots, gain, scale, layer_mult, back.reshape(n_experts * 8, width // 2))
    return result[None, None]


def solution(mesh):
    rows = P("dp", "expert", None)
    in_specs = (P("dp", "expert", None, None),) * 5 + (P("dp", "expert"),) + (rows,) * 3 + (
        P(), P("expert", None, "dp"), P("expert", None, "dp"), P(),
    )
    out_specs = P("dp", "expert", None, None)
    return jax.shard_map(body, mesh=mesh, in_specs=in_specs, out_specs=out_specs, check_vma=False)
```

```python
import math

import jax
import jax.numpy as jnp
from jax import lax
from jax.experimental import pallas as pl
from jax.experimental.pallas import tpu as pltpu
from jax.sharding import PartitionSpec as P

HEAD_DIM = 64
NT = (((1,), (1,)), ((), ()))
F32 = jnp.float32
BF16 = jnp.bfloat16


def mm(lhs, rhs):
    return jnp.dot(lhs, rhs, preferred_element_type=F32)


def mm_nt(lhs, rhs):
    return lax.dot_general(lhs, rhs, NT, preferred_element_type=F32)


def column_of(row):
    n = row.shape[1]
    eye = lax.broadcasted_iota(jnp.int32, (n, n), 0) == lax.broadcasted_iota(jnp.int32, (n, n), 1)
    return jnp.sum(jnp.where(eye, jnp.broadcast_to(row, (n, n)), 0.0), axis=1, keepdims=True)


def prepare_kernel(
    length_ref, ids_hbm, slots_hbm, gate_hbm, gain_hbm, enc_hbm, base_hbm, keys_hbm, query_hbm, mult_hbm, wv_hbm,
    placed_ref, layer_ref, scale_ref,
    ids_ref, slots_ref, gate_ref, gain_ref, enc_ref, base_ref, keys_ref, query_ref, mult_ref, wv_ref, value_ref, sems,
):
    enc_len, width = enc_ref.shape
    dec_len = query_ref.shape[0]
    copies = [
        pltpu.make_async_copy(src, dst, sems.at[i])
        for i, (src, dst) in enumerate(
            (
                (keys_hbm, keys_ref), (query_hbm, query_ref), (mult_hbm, mult_ref),
                (wv_hbm, wv_ref), (enc_hbm, enc_ref), (base_hbm, base_ref),
                (ids_hbm, ids_ref), (slots_hbm, slots_ref), (gate_hbm, gate_ref), (gain_hbm, gain_ref),
            )
        )
    ]
    for copy in copies:
        copy.start()
    for copy in copies[:3]:
        copy.wait()
    first = lax.broadcasted_iota(jnp.int32, (dec_len, 2 * HEAD_DIM), 1) < HEAD_DIM
    valid = lax.broadcasted_iota(jnp.int32, (enc_len, 2 * dec_len), 0) < length_ref[0, 0]
    for pair in range(width // (2 * HEAD_DIM)):
        lanes = slice(pair * 2 * HEAD_DIM, (pair + 1) * 2 * HEAD_DIM)
        query, mult = query_ref[:, lanes], mult_ref[:, lanes]
        zeros = jnp.zeros_like(query)
        queries = jnp.concatenate([jnp.where(first, query, zeros), jnp.where(first, zeros, query)], axis=0)
        mults = jnp.concatenate([jnp.where(first, mult, zeros), jnp.where(first, zeros, mult)], axis=0)
        scores = mm_nt(keys_ref[:, lanes], queries) * (1.0 / math.sqrt(HEAD_DIM))
        scores = jnp.where(valid, scores, -jnp.inf)
        expo = jnp.exp(scores - jnp.max(scores, axis=0, keepdims=True))
        attn = (expo * (1.0 / jnp.sum(expo, axis=0, keepdims=True))).astype(BF16)
        value_ref[:, lanes] = mm(attn, mults).astype(BF16)
    copies[3].wait()
    for copy in copies[6:]:
        copy.wait()
    layer_mult = mm_nt(value_ref[...], wv_ref[...])
    layer_ref[...] = layer_mult
    scaled_mult = (column_of(gate_ref[...]) * layer_mult).astype(BF16)
    copies[4].wait()
    copies[5].wait()
    tokens = enc_ref[...].astype(F32)
    inv = lax.rsqrt(jnp.mean(tokens * tokens, axis=-1, keepdims=True) + 1e-06)
    scale_ref[...] = jnp.broadcast_to(inv, scale_ref.shape)
    row_scale = gain_ref[...] * inv
    inputs = (tokens * row_scale).astype(BF16)
    base_inputs = (base_ref[...].astype(F32) * row_scale).astype(BF16)
    half = width // 2
    row = ids_ref[...] * 8 + slots_ref[...]
    at = lax.broadcasted_iota(jnp.int32, (placed_ref.shape[0], enc_len), 0)
    low = jnp.where(at == row, 1.0, 0.0).astype(BF16)
    high = jnp.where(at == row + 4, 1.0, 0.0).astype(BF16)
    placed_ref[:, :half] = (mm(low, inputs[:, :half]) + mm(high, inputs[:, half:])).astype(BF16)
    placed_ref[:, half:width] = (mm(low, base_inputs[:, :half]) + mm(high, base_inputs[:, half:])).astype(BF16)
    placed_ref[:, width:] = (mm(low, scaled_mult[:, :half]) + mm(high, scaled_mult[:, half:])).astype(BF16)


def prepare(length, ids, slots, gate, gain, enc, base, keys, query, mult, wv, n_rows):
    enc_len, width = enc.shape
    vmem = pl.BlockSpec(memory_space=pltpu.VMEM)
    taken = (ids, slots, gate, gain, enc, base, keys, query, mult, wv)
    return pl.pallas_call(
        prepare_kernel,
        in_specs=[pl.BlockSpec(memory_space=pltpu.SMEM)] + [pl.BlockSpec(memory_space=pltpu.HBM)] * len(taken),
        out_specs=[vmem] * 3,
        out_shape=[
            jax.ShapeDtypeStruct((n_rows, 3 * width // 2), BF16),
            jax.ShapeDtypeStruct((enc_len, width), F32),
            jax.ShapeDtypeStruct((enc_len, 128), F32),
        ],
        scratch_shapes=[pltpu.VMEM(a.shape, a.dtype) for a in taken]
        + [pltpu.VMEM((enc_len, width), BF16), pltpu.SemaphoreType.DMA((len(taken),))],
        compiler_params=pltpu.CompilerParams(vmem_limit_bytes=62 << 20),
        name="prepare",
    )(length, *taken)


def rescale(pre_act, base_act):
    upper_part = jnp.maximum(jnp.maximum(pre_act, base_act), 0.0)
    lower_part = jnp.maximum(-jnp.minimum(pre_act, base_act), 0.0)
    return upper_part / (upper_part + lower_part + jnp.where(upper_part > 0.0, 0.0, 1.0))


def hidden_blocks(length, block=256):
    return [slice(at, min(at + block, length)) for at in range(0, length, block)]


def first_kernel(
    rows_hbm, kept_in, kept_in2, kept_out, kept_out2, last_in, last_in2,
    partial_ref, ratio_ref, mult_ref, rows_ref, in_ref, w_in_ref, w_out_ref, act_ref, sems,
):
    n_tiles, _, lanes = rows_ref.shape
    half = lanes // 3
    n_rows = n_tiles * 4
    part_len = kept_in.shape[0]
    hidden = 2 * part_len

    def part(src, dst, i, sem):
        return pltpu.make_async_copy(src, dst.at[pl.ds(i * part_len, part_len)], sems.at[sem])

    copies = [
        part(kept_in, w_in_ref, 0, 0), part(kept_out, w_out_ref, 0, 1), part(kept_in2, w_in_ref, 1, 2),
        part(kept_out2, w_out_ref, 1, 3), part(last_in, w_in_ref, 2, 4), part(last_in2, w_in_ref, 3, 5),
    ]
    row_copies = []
    for i in range(3):
        lanes_of = (slice(None), slice(None), pl.ds(i * half, half))
        row_copies.append(pltpu.make_async_copy(rows_hbm.at[lanes_of], rows_ref.at[lanes_of], sems.at[6 + i]))
    for copy in [*row_copies[:2], copies[0], row_copies[2], *copies[1:]]:
        copy.start()
    upper_rows = lax.broadcasted_iota(jnp.int32, (n_tiles // 2, 8, half), 1) < 4
    for i, ref in enumerate((in_ref.at[:n_rows], in_ref.at[n_rows:], mult_ref)):
        row_copies[i].wait()
        block = rows_ref[:, :, i * half : (i + 1) * half].astype(F32).reshape(n_tiles // 2, 2, 8, half)
        even, odd = block[:, 0], block[:, 1]
        low = jnp.where(upper_rows, even, pltpu.roll(odd, 4, 1))
        high = jnp.where(upper_rows, pltpu.roll(even, 4, 1), odd)
        ref[:, :half] = low.reshape(n_rows, half).astype(BF16)
        ref[:, half:] = high.reshape(n_rows, half).astype(BF16)
    for copy in copies[:2]:
        copy.wait()
    for i, cols in enumerate(hidden_blocks(hidden)):
        if i == part_len // 256:
            for copy in copies[2:4]:
                copy.wait()
        both = mm_nt(in_ref[...], w_in_ref[cols, :])
        hidden_mult = mm_nt(mult_ref[...], w_out_ref[cols, :])
        act_ref[:, cols] = (rescale(both[:n_rows], both[n_rows:]) * hidden_mult).astype(BF16)
    for copy in copies[4:]:
        copy.wait()
    for cols in hidden_blocks(hidden):
        both = mm_nt(in_ref[...], w_in_ref[slice(hidden + cols.start, hidden + cols.stop), :])
        ratio_ref[:, cols] = rescale(both[:n_rows], both[n_rows:])
    partial_ref[...] = mm(act_ref[...], w_in_ref[:hidden, :])


def last_kernel(
    mult_hbm, partial_hbm, ratio_hbm, last_in, last_in2, last_out, last_out2,
    out_ref, mult_ref, partial_ref, ratio_ref, w_in_ref, w_out_ref, act_ref, sems,
):
    n_rows, width = mult_hbm.shape
    half = width // 2
    n_tiles = n_rows // 4
    part_len = last_in.shape[0]
    hidden = 2 * part_len

    def part(src, dst, i, sem):
        return pltpu.make_async_copy(src, dst.at[pl.ds(i * part_len, part_len)], sems.at[sem])

    def ratio_part(lanes, sem):
        return pltpu.make_async_copy(ratio_hbm.at[:, lanes], ratio_ref.at[:, lanes], sems.at[sem])

    copies = [
        part(last_out, w_out_ref, 0, 0), pltpu.make_async_copy(mult_hbm, mult_ref, sems.at[1]),
        ratio_part(pl.ds(0, 512), 2), part(last_out2, w_out_ref, 1, 3), ratio_part(pl.ds(512, hidden - 512), 4),
        part(last_in, w_in_ref, 0, 5), part(last_in2, w_in_ref, 1, 6),
        pltpu.make_async_copy(partial_hbm, partial_ref, sems.at[7]),
    ]
    for copy in copies:
        copy.start()
    for copy in copies[:3]:
        copy.wait()
    for i, cols in enumerate(hidden_blocks(hidden)):
        if i == 2:
            for copy in copies[3:5]:
                copy.wait()
        act_ref[:, cols] = (ratio_ref[:, cols] * mm_nt(mult_ref[...], w_out_ref[cols, :])).astype(BF16)
    for copy in copies[5:]:
        copy.wait()
    upper_rows = lax.broadcasted_iota(jnp.int32, (n_tiles // 2, 8, half), 1) < 4
    low = (partial_ref[:, :half] + mm(act_ref[...], w_in_ref[:, :half])).reshape(n_tiles // 2, 8, half)
    high = (partial_ref[:, half:] + mm(act_ref[...], w_in_ref[:, half:])).reshape(n_tiles // 2, 8, half)
    out_ref[:, 0] = jnp.where(upper_rows, low, pltpu.roll(high, 4, 1)).astype(BF16)
    out_ref[:, 1] = jnp.where(upper_rows, pltpu.roll(low, 4, 1), high).astype(BF16)


def expert_first(rows, weights):
    n_tiles, _, lanes = rows.shape
    n_rows, width = n_tiles * 4, 2 * lanes // 3
    hidden = 2 * weights[0].shape[0]
    return pl.pallas_call(
        first_kernel,
        in_specs=[pl.BlockSpec(memory_space=pltpu.HBM)] * 7,
        out_specs=[pl.BlockSpec(memory_space=pltpu.VMEM)] * 3,
        out_shape=[
            jax.ShapeDtypeStruct((n_rows, width), F32), jax.ShapeDtypeStruct((n_rows, hidden), F32),
            jax.ShapeDtypeStruct((n_rows, width), BF16),
        ],
        scratch_shapes=[
            pltpu.VMEM(rows.shape, BF16), pltpu.VMEM((2 * n_rows, width), BF16),
            pltpu.VMEM((2 * hidden, width), BF16), pltpu.VMEM((hidden, width), BF16),
            pltpu.VMEM((n_rows, hidden), BF16), pltpu.SemaphoreType.DMA((9,)),
        ],
        compiler_params=pltpu.CompilerParams(vmem_limit_bytes=62 << 20),
        name="expert_first",
    )(rows, *weights)


def expert_last(mult, partial, ratio, weights):
    n_rows, width = mult.shape
    hidden = ratio.shape[1]
    return pl.pallas_call(
        last_kernel,
        in_specs=[pl.BlockSpec(memory_space=pltpu.HBM)] * 6 + [pl.BlockSpec(memory_space=pltpu.VMEM)],
        out_specs=pl.BlockSpec(memory_space=pltpu.VMEM),
        out_shape=jax.ShapeDtypeStruct((n_rows // 8, 2, 8, width // 2), BF16),
        scratch_shapes=[
            pltpu.VMEM(mult.shape, BF16), pltpu.VMEM((n_rows, width), F32), pltpu.VMEM((n_rows, hidden), F32),
            pltpu.VMEM((hidden, width), BF16), pltpu.VMEM((hidden, width), BF16),
            pltpu.VMEM((n_rows, hidden), BF16), pltpu.SemaphoreType.DMA((8,)),
        ],
        compiler_params=pltpu.CompilerParams(vmem_limit_bytes=58 << 20),
        name="expert_last",
    )(mult, partial, ratio, *weights)


def combine_kernel(ids_ref, slots_ref, gain_ref, scale_ref, layer_ref, back_ref, out_ref):
    enc_len, width = layer_ref.shape
    half = width // 2
    row = column_of((ids_ref[...] * 8 + slots_ref[...]).astype(F32)).astype(jnp.int32)
    at = lax.broadcasted_iota(jnp.int32, (enc_len, back_ref.shape[0]), 1)
    row_scale = gain_ref[...] * scale_ref[:, :1]
    for i in range(2):
        lanes = slice(i * half, (i + 1) * half)
        chosen = jnp.where(at == row + 4 * i, 1.0, 0.0).astype(BF16)
        per_token = mm(chosen, back_ref[...])
        out_ref[:, lanes] = (layer_ref[:, lanes] + row_scale[:, lanes] * per_token).astype(BF16)


def combine(ids, slots, gain, scale, layer_mult, back):
    return pl.pallas_call(
        combine_kernel,
        in_specs=[pl.BlockSpec(memory_space=pltpu.VMEM)] * 6,
        out_specs=pl.BlockSpec(memory_space=pltpu.VMEM),
        out_shape=jax.ShapeDtypeStruct(layer_mult.shape, BF16),
        compiler_params=pltpu.CompilerParams(vmem_limit_bytes=32 << 20),
        name="combine",
    )(ids, slots, gain, scale, layer_mult, back)


def expert_layer(w_in, w_out_t, rows, n_expert_devices):
    axes = ("expert", "dp")
    first_round, second_round = [], []
    for chip in range(n_expert_devices // 2):
        for core in range(2):
            for at in range(4):
                home = at // 2
                here = (chip * 2 + core) * 4 + at
                if core == home:
                    first_to, first_core = at ^ 1, 1 - home
                    second_to, second_core = at ^ 1, home
                else:
                    first_to, first_core = 3 - at, core
                    second_to, second_core = 3 - at, 1 - core
                first_round.append((here, (chip * 2 + first_core) * 4 + first_to))
                second_round.append((here, (chip * 2 + second_core) * 4 + second_to))
    at = lax.axis_index("dp")
    is_home = (at // 2) == (lax.axis_index("expert") % 2)
    first = jnp.where(is_home, 1 - at % 2, at % 2)
    w_in, w_out_t = jnp.swapaxes(w_in, 1, 2), jnp.swapaxes(w_out_t, 1, 2)

    swap = [(i, i ^ 1) for i in range(n_expert_devices)]
    kept, last = [], []
    for weights in (w_in, w_out_t):
        came = lax.ppermute(lax.dynamic_index_in_dim(weights, first, 0, keepdims=False), axes, first_round)
        came, late = lax.optimization_barrier((came, weights))
        rest = lax.dynamic_index_in_dim(late, 1 - first, 0, keepdims=False)
        kept.append(jnp.where(is_home, rest, came))
        last.append(lax.ppermute(jnp.where(is_home, came, rest), axes, second_round))
    kept = lax.optimization_barrier(kept)
    other = []
    for piece in [*kept, last[0]]:
        if other:
            other[-1], piece = lax.optimization_barrier((other[-1], piece))
        other.append(lax.ppermute(piece, "expert", swap))
    partial, ratio, mult = expert_first(rows, [kept[0], other[0], kept[1], other[1], last[0], other[2]])
    partial, final = lax.optimization_barrier((partial, last[1]))
    return expert_last(mult, partial, ratio, [last[0], other[2], final, lax.ppermute(final, "expert", swap)])


def body(
    enc_state, baseline, enc_keys, dec_queries, out_mult, doc_lengths, expert_ids, slot_ids, gate_prob, norm_gain,
    w_in, w_out_t, w_value,
):
    enc_len, width = enc_state.shape[2:]
    n_expert_devices = lax.axis_size("expert")
    n_experts = w_in.shape[0] * n_expert_devices
    axes = ("expert", "dp")
    groups = [
        [(chip * 2 + core) * 4 + at for chip in range(n_expert_devices // 2) for at in range(4)] for core in range(2)
    ]

    def exchange(rows):
        return lax.all_to_all(rows, axes, split_axis=0, concat_axis=0, axis_index_groups=groups, tiled=True)

    ids, slots, gain = expert_ids[0], slot_ids[0], norm_gain[None, :]
    placed, layer_mult, scale = prepare(
        doc_lengths, ids, slots, gate_prob[0], gain, enc_state[0, 0], baseline[0, 0], enc_keys[0, 0],
        dec_queries[0, 0], out_mult[0, 0], w_value, n_experts * 8,
    )
    came = exchange(placed.reshape(n_experts, 8, 3 * width // 2))
    slot_mult = expert_layer(w_in, w_out_t, came, n_expert_devices)
    back = exchange(slot_mult.reshape(n_experts, 8, width // 2))
    result = combine(ids, slots, gain, scale, layer_mult, back.reshape(n_experts * 8, width // 2))
    return result[None, None]


def solution(mesh):
    rows = P("dp", "expert", None)
    in_specs = (P("dp", "expert", None, None),) * 5 + (P("dp", "expert"),) + (rows,) * 3 + (
        P(), P("expert", None, "dp"), P("expert", None, "dp"), P(),
    )
    out_specs = P("dp", "expert", None, None)
    return jax.shard_map(body, mesh=mesh, in_specs=in_specs, out_specs=out_specs, check_vma=False)
```
